32 devices in a mesh: walker: 2 (over core), slab: 2 (over x), chol: 8 (over z, y).
Axes of the slice: x: 2, y: 2, z: 4, core: 2. Of those that a mesh axis runs over, the one named last changes fastest.
Arguments:
- cholesky_factors: bfloat16 [96, 256, 2048], P('chol', None, 'slab'), may hold values from -0.13183594 to 0.13183594
- greens: bfloat16 [2, 256, 2048], P('walker', 'chol', 'slab'), may hold values from -1.7265625 to 1.7265625
- walker_weights: float32 [2], P('walker'), may hold values from 0.3 to 3
Outputs:
- fock: float32 [256, 2048], P(('walker', 'chol'), 'slab')
The draws below stay inside these ranges and needn't reach their ends.
All inputs are finite; a program needn't handle non-finite values.
Results may differ from the reference program's by a relative error of at most 0.0029.
Values may be sent and summed in bfloat16 or wider, within the bound.
A program may use at most 64 MiB of HBM per device.

```python
import math
import jax
import jax.numpy as jnp
from jax import lax

NORB = 2048
OCCUPIED_COUNT = 256
CHOLESKY_COUNT = 96
WALKERS = 2


def shard_levels(own_key, dims, split, smallest, largest):
    loudness = 1.0
    for axis_at, parts in split:
        steps = jax.random.uniform(jax.random.fold_in(jax.random.fold_in(own_key, 6), axis_at), (parts,), jnp.float32, smallest / len(split), largest / len(split))
        loudness = loudness * jnp.repeat(jnp.exp(steps), dims[axis_at] // parts).reshape((-1,) + (1,) * (len(dims) - 1 - axis_at))
    return loudness


def noise(key, extent, spread, most, cuts=(), kind=jnp.bfloat16):
    values = jax.random.normal(key, extent, jnp.float32) * spread
    if len(cuts) > 0:
        values = shard_levels(key, extent, cuts, -0.22, 0.18) * values
    return jnp.clip(values, min=-most, max=most).astype(kind)


def setup_inputs(seed: int = 0) -> dict:
    keys = jax.random.split(jax.random.key(seed), 4)
    cholesky_factors = noise(keys[0], (CHOLESKY_COUNT, OCCUPIED_COUNT, NORB), (NORB ** -0.5), 0.13183594, ((0, 8), (2, 2)))
    greens = noise(keys[1], (WALKERS, OCCUPIED_COUNT, NORB), ((NORB * 1.0) ** 0.5 * (OCCUPIED_COUNT * CHOLESKY_COUNT) ** -0.5), 1.7265625, ((0, 2), (1, 8), (2, 2)))
    walker_weights = jnp.clip(jnp.exp(math.log(3.0) - 2.3025851 * jax.random.uniform(keys[2], (WALKERS,), jnp.float32) ** shard_levels(keys[2], (WALKERS,), ((0, 2),), -0.2, 0.2)), 0.3, 3.0)
    return dict(cholesky_factors=cholesky_factors, greens=greens, walker_weights=walker_weights)


def reference(cholesky_factors, greens, walker_weights):
    factors_wide = cholesky_factors.astype(jnp.float32)

    def one_walker(inputs):
        theta, weight = inputs
        margin = jnp.einsum("gnp,mp->gnm", factors_wide, theta.astype(jnp.float32)).astype(jnp.bfloat16)
        terms = jnp.einsum("gnm,gmp->np", margin.astype(jnp.float32), factors_wide)
        return weight * terms

    per_walker = lax.map(one_walker, (greens, walker_weights))
    return jnp.sum(per_walker, axis=0)
```

```python
import functools

import jax
import jax.numpy as jnp
from jax import lax
from jax.experimental import pallas as pl
from jax.experimental.pallas import tpu as pltpu
from jax.sharding import PartitionSpec as P

MESH = pl.DeviceIdType.MESH
NT = (((1,), (1,)), ((), ()))


def exchange_kernel(
    sizes, l_hbm, theta_ref, weight_ref, out_ref,
    lv, th, wbuf, own, sbuf, rbuf, fsend, frecv,
    l_sem, w_sem, z_send, y_send, c_send, th_recv, x_send, x_recv, f_send, f_recv,
):
    n_chol, vectors, occupied, block_rows = sizes
    n_hi = n_chol // 2
    half = occupied // 2
    chunk_rows = 2 * block_rows
    n_chunks = n_hi
    w = lax.axis_index("walker")
    s = lax.axis_index("slab")
    me = lax.axis_index("chol")
    z, y = me // 2, me % 2
    sibling = {"walker": 1 - w}
    peer = {"slab": 1 - s}
    y_peer = {"chol": z * 2 + 1 - y}

    mine = pl.ds(pl.multiple_of(w * half, half), half)
    other = pl.ds(pl.multiple_of((1 - w) * half, half), half)
    load_mine = pltpu.make_async_copy(l_hbm.at[:, mine], lv.at[:, mine], l_sem.at[0])
    load_other = pltpu.make_async_copy(l_hbm.at[:, other], lv.at[:, other], l_sem.at[1])
    load_mine.start()
    load_other.start()
    wbuf[w] = jnp.full(wbuf.shape[1:], weight_ref[0], jnp.float32)

    barrier = pltpu.get_barrier_semaphore()
    for k in range(1, n_chol):
        pl.semaphore_signal(
            barrier, inc=1, device_id={"chol": lax.rem(me + k, n_chol)}, device_id_type=MESH
        )
    pl.semaphore_signal(barrier, inc=1, device_id=sibling, device_id_type=MESH)
    pl.semaphore_signal(barrier, inc=1, device_id=peer, device_id_type=MESH)
    pl.semaphore_wait(barrier, n_chol + 1)

    def rdma(src, dst, send, recv, to):
        return pltpu.make_async_remote_copy(
            src_ref=src, dst_ref=dst, send_sem=send, recv_sem=recv, device_id=to, device_id_type=MESH
        )

    sends = []

    def send(src, block, sem, to):
        copy = rdma(src, th.at[w, block], sem, th_recv.at[w, block], to)
        copy.start()
        sends.append(copy)

    def arrived(walker, block):
        rdma(th.at[walker, block], th.at[walker, block], c_send.at[0], th_recv.at[walker, block], sibling).wait_recv()

    first = theta_ref.at[0]
    send(first, me, y_send.at[0], y_peer)
    order = sorted(range(1, n_hi), key=lambda d: min(d, n_hi - d))
    for d in order:
        send(first, me, z_send.at[d], {"chol": lax.rem(z + d, n_hi) * 2 + y})
    send(first, me, c_send.at[0], sibling)
    weights = rdma(wbuf.at[w], wbuf.at[w], w_sem.at[0], w_sem.at[1], sibling)
    weights.start()
    th[w, me] = theta_ref[0]
    count = 1
    for i, d in enumerate(order):
        block = lax.rem(z + n_hi - d, n_hi) * 2 + y
        arrived(w, block)
        send(th.at[w, block], block, y_send.at[1 + i], y_peer)
        send(th.at[w, block], block, c_send.at[count], sibling)
        count += 1
    for d in [0] + order:
        block = lax.rem(z + n_hi - d, n_hi) * 2 + 1 - y
        arrived(w, block)
        send(th.at[w, block], block, c_send.at[count], sibling)
        count += 1
    for block in range(n_chol):
        arrived(1 - w, block)
    rdma(wbuf.at[1 - w], wbuf.at[1 - w], w_sem.at[0], w_sem.at[1], sibling).wait_recv()
    load_mine.wait()

    def margins(t, carry):
        at = lax.rem(z + 1 + t, n_hi)
        rows = pl.ds(pl.multiple_of(w * half + at * chunk_rows, chunk_rows), chunk_rows)
        x = lv[:, rows, :].reshape(vectors * chunk_rows, -1)
        a = 0.0
        for k in range(2):
            part = lax.dot_general(
                x, th[k].reshape(occupied, -1), NT, preferred_element_type=jnp.float32
            )
            a = a + wbuf[k][:1, :1] * part
        own[t] = a
        sbuf[t] = a.astype(jnp.bfloat16)
        rdma(sbuf.at[t], rbuf.at[t], x_send.at[t], x_recv.at[t], peer).start()
        return carry

    lax.fori_loop(0, n_chunks, margins, 0)
    load_other.wait()

    def fock(t, carry):
        at = lax.rem(z + 1 + t, n_hi)
        rdma(sbuf.at[t], rbuf.at[t], x_send.at[t], x_recv.at[t], peer).wait_recv()
        total = own[t] + rbuf[t].astype(jnp.float32)
        total = jnp.concatenate(
            [total[g * chunk_rows : (g + 1) * chunk_rows] for g in range(vectors)], axis=1
        )
        high = total.astype(jnp.bfloat16)
        low = (total - high.astype(jnp.float32)).astype(jnp.bfloat16)
        both = jnp.dot(
            jnp.concatenate([high, low], axis=0),
            lv[...].reshape(vectors * occupied, -1),
            preferred_element_type=jnp.float32,
        )
        f = both[:chunk_rows] + both[chunk_rows:]
        for d in range(2):
            fsend[t, d] = f[d * block_rows : (d + 1) * block_rows]
            to = at * 2 + d

            @pl.when(to != me)
            def _():
                rdma(fsend.at[t, d], frecv.at[me], f_send.at[t, d], f_recv.at[me], {"chol": to}).start()

        return carry

    lax.fori_loop(0, n_chunks, fock, 0)

    result = fsend[n_chunks - 1, y]
    for k in range(1, n_chol):
        source = lax.rem(me + k, n_chol)
        rdma(frecv.at[source], frecv.at[source], f_send.at[0, 0], f_recv.at[source], sibling).wait_recv()
        result = result + frecv[source]
    out_ref[...] = result

    for copy in sends:
        copy.wait_send()
    weights.wait_send()

    def drain(t, carry):
        at = lax.rem(z + 1 + t, n_hi)
        rdma(sbuf.at[t], rbuf.at[t], x_send.at[t], x_recv.at[t], peer).wait_send()
        for d in range(2):

            @pl.when(at * 2 + d != me)
            def _():
                rdma(fsend.at[t, d], frecv.at[me], f_send.at[t, d], f_recv.at[me], peer).wait_send()

        return carry

    lax.fori_loop(0, n_chunks, drain, 0)


def fused(n_chol, cholesky_factors, greens, walker_weights):
    vectors, occupied, orbitals = cholesky_factors.shape
    theta_rows = greens.shape[1]
    block_rows = occupied // (2 * n_chol)
    n_hi = n_chol // 2
    rows = vectors * 2 * block_rows
    dma = pltpu.SemaphoreType.DMA
    return pl.pallas_call(
        functools.partial(exchange_kernel, (n_chol, vectors, occupied, block_rows)),
        out_shape=jax.ShapeDtypeStruct((block_rows, orbitals), jnp.float32),
        in_specs=[
            pl.BlockSpec(memory_space=pl.ANY),
            pl.BlockSpec(memory_space=pltpu.VMEM),
            pl.BlockSpec(memory_space=pltpu.SMEM),
        ],
        out_specs=pl.BlockSpec(memory_space=pltpu.VMEM),
        scratch_shapes=[
            pltpu.VMEM((vectors, occupied, orbitals), jnp.bfloat16),
            pltpu.VMEM((2, n_chol, theta_rows, orbitals), jnp.bfloat16),
            pltpu.VMEM((2, 8, 128), jnp.float32),
            pltpu.VMEM((n_hi, rows, occupied), jnp.float32),
            pltpu.VMEM((n_hi, rows, occupied), jnp.bfloat16),
            pltpu.VMEM((n_hi, rows, occupied), jnp.bfloat16),
            pltpu.VMEM((n_hi, 2, block_rows, orbitals), jnp.float32),
            pltpu.VMEM((n_chol, block_rows, orbitals), jnp.float32),
            dma((2,)),
            dma((2,)),
            dma((n_hi,)),
            dma((n_hi,)),
            dma((n_chol,)),
            dma((2, n_chol)),
            dma((n_hi,)),
            dma((n_hi,)),
            dma((n_hi, 2)),
            dma((n_chol,)),
        ],
        compiler_params=pltpu.CompilerParams(collective_id=0, has_side_effects=True),
    )(cholesky_factors, greens, walker_weights)


def plain(cholesky_factors, greens, walker_weights):
    panel_sum_terms = jnp.einsum(
        "gnp,mp->gnm",
        cholesky_factors,
        lax.all_gather(greens[0], "chol", axis=0, tiled=True),
        preferred_element_type=jnp.float32,
    )
    margin = lax.psum(panel_sum_terms, "slab").astype(jnp.bfloat16)
    terms = jnp.einsum("gnm,gmp->np", margin, cholesky_factors, preferred_element_type=jnp.float32)
    weighted = walker_weights[0] * terms
    return lax.psum_scatter(weighted, ("walker", "chol"), scatter_dimension=0, tiled=True)


def solution(mesh):
    walkers, slabs, n_chol = (mesh.shape[axis] for axis in ("walker", "slab", "chol"))

    def per_device(cholesky_factors, greens, walker_weights):
        occupied = cholesky_factors.shape[1]
        pair = walkers == 2 and slabs == 2 and greens.shape[0] == 1
        if pair and n_chol % 2 == 0 and occupied % (16 * n_chol) == 0:
            return fused(n_chol, cholesky_factors, greens, walker_weights)
        return plain(cholesky_factors, greens, walker_weights)

    in_specs = (P("chol", None, "slab"), P("walker", "chol", "slab"), P("walker"))
    out_specs = P(("walker", "chol"), "slab")
    return jax.shard_map(
        per_device, mesh=mesh, in_specs=in_specs, out_specs=out_specs, check_vma=False
    )
```

```python
import functools

import jax
import jax.numpy as jnp
from jax import lax
from jax.experimental import pallas as pl
from jax.experimental.pallas import tpu as pltpu
from jax.sharding import PartitionSpec as P

MESH = pl.DeviceIdType.MESH
NT = (((1,), (1,)), ((), ()))


def exchange_kernel(
    sizes, l_hbm, theta_hbm, weight_ref, out_ref,
    lv, th, wbuf, own, sbuf, rbuf, fsend, frecv,
    l_sem, w_sem, z_send, y_send, c_send, th_recv, x_send, x_recv, f_send, f_recv,
):
    n_chol, vectors, occupied, block_rows = sizes
    n_hi = n_chol // 2
    half = occupied // 2
    chunk_rows = 2 * block_rows
    n_chunks = n_hi
    n_groups = n_hi // 2
    w = lax.axis_index("walker")
    s = lax.axis_index("slab")
    me = lax.axis_index("chol")
    z, y = me // 2, me % 2
    step = 1 - 2 * (z % 2)
    sibling = {"walker": 1 - w}
    peer = {"slab": 1 - s}
    y_peer = {"chol": z * 2 + 1 - y}

    def line(at):
        return jnp.logical_and(at >= 0, at < n_hi)

    def signal(to):
        pl.semaphore_signal(barrier, inc=1, device_id=to, device_id_type=MESH)

    barrier = pltpu.get_barrier_semaphore()
    signal(sibling)
    signal(y_peer)
    signal({"chol": (z + step) * 2 + y})
    signal(peer)

    @pl.when(line(z - step))
    def _():
        signal({"chol": (z - step) * 2 + y})

    mine = pl.ds(pl.multiple_of(w * half, half), half)
    other = pl.ds(pl.multiple_of((1 - w) * half, half), half)
    keep = pltpu.make_async_copy(theta_hbm.at[0], th.at[w, me], l_sem.at[2])
    load_mine = pltpu.make_async_copy(l_hbm.at[:, mine], lv.at[:, mine], l_sem.at[0])
    load_other = pltpu.make_async_copy(l_hbm.at[:, other], lv.at[:, other], l_sem.at[1])
    keep.start()
    wbuf[w] = jnp.full(wbuf.shape[1:], weight_ref[0], jnp.float32)
    keep.wait()

    pl.semaphore_wait(barrier, 4 + line(z - step).astype(jnp.int32))

    def rdma(src, dst, send, recv, to):
        return pltpu.make_async_remote_copy(
            src_ref=src, dst_ref=dst, send_sem=send, recv_sem=recv, device_id=to, device_id_type=MESH
        )

    def pass_on(block, sem, to):
        return rdma(th.at[w, block], th.at[w, block], sem.at[block], th_recv.at[w, block], to)

    def arrived(walker, block):
        rdma(th.at[walker, block], th.at[walker, block], c_send.at[0], th_recv.at[walker, block], sibling).wait_recv()

    def relay(block, onward):
        @pl.when(line(onward))
        def _():
            pass_on(block, z_send, {"chol": onward * 2 + y}).start()

        pass_on(block, y_send, y_peer).start()
        pass_on(block, c_send, sibling).start()

    def from_line(d, way):
        at = z + way * d

        @pl.when(line(at))
        def _():
            arrived(w, at * 2 + y)
            relay(at * 2 + y, z - way)

    def from_y(at):
        @pl.when(line(at))
        def _():
            arrived(w, at * 2 + 1 - y)
            pass_on(at * 2 + 1 - y, c_send, sibling).start()

    @pl.when(line(z - step))
    def _():
        rdma(th.at[w, me], th.at[w, me], z_send.at[n_chol], th_recv.at[w, me], {"chol": (z - step) * 2 + y}).start()

    relay(me, z + step)
    weights = rdma(wbuf.at[w], wbuf.at[w], w_sem.at[0], w_sem.at[1], sibling)
    weights.start()
    load_mine.start()
    load_other.start()
    from_line(1, step)
    from_line(1, -step)
    from_y(z)
    from_y(z + step)
    from_line(2, step)
    from_line(2, -step)

    def margins(t, q):
        at = lax.rem(z + 1 + t, n_hi)
        rows = pl.ds(pl.multiple_of(w * half + at * chunk_rows, chunk_rows), chunk_rows)
        x = lv[:, rows, :].reshape(vectors * chunk_rows, -1)
        theta = th[:, pl.ds(4 * q, 4)]
        width = 4 * theta.shape[2]
        both = lax.dot_general(
            x, theta.reshape(2 * width, -1), NT, preferred_element_type=jnp.float32
        )
        a = wbuf[0][:1, :1] * both[:, :width] + wbuf[1][:1, :1] * both[:, width:]
        own[t, q] = a
        sbuf[t, q] = a.astype(jnp.bfloat16)
        rdma(sbuf.at[t, q], rbuf.at[t, q], x_send.at[t, q], x_recv.at[t, q], peer).start()

    def group_arrived(q):
        for k in range(4):
            arrived(1 - w, 4 * q + k)

    def some_margins(first, last, q):
        def body(t, carry):
            margins(t, q)
            return carry

        lax.fori_loop(first, last, body, 0)

    here = z // 2
    group_arrived(here)
    rdma(wbuf.at[1 - w], wbuf.at[1 - w], w_sem.at[0], w_sem.at[1], sibling).wait_recv()
    load_mine.wait()
    some_margins(0, n_chunks - 1, here)
    for d in range(3, n_hi):
        from_line(d, step)
        from_line(d, -step)
    from_y(z - step)
    for d in range(2, n_hi):
        from_y(z + d * step)
        from_y(z - d * step)
    for k in range(1, n_groups):
        q = lax.rem(here + k, n_groups)
        group_arrived(q)
        some_margins(0, n_chunks - 1, q)
    for k in range(n_groups):
        some_margins(n_chunks - 1, n_chunks, lax.rem(here + k, n_groups))
    load_other.wait()

    def fock(t, carry):
        at = lax.rem(z + 1 + t, n_hi)
        totals = []
        for q in range(n_groups):
            rdma(sbuf.at[t, q], rbuf.at[t, q], x_send.at[t, q], x_recv.at[t, q], peer).wait_recv()
        for q in range(n_groups):
            totals.append(own[t, q] + rbuf[t, q].astype(jnp.float32))
        total = jnp.concatenate(
            [
                total[g * chunk_rows : (g + 1) * chunk_rows]
                for g in range(vectors)
                for total in totals
            ],
            axis=1,
        )
        high = total.astype(jnp.bfloat16)
        low = (total - high.astype(jnp.float32)).astype(jnp.bfloat16)
        both = jnp.dot(
            jnp.concatenate([high, low], axis=0),
            lv[...].reshape(vectors * occupied, -1),
            preferred_element_type=jnp.float32,
        )
        f = both[:chunk_rows] + both[chunk_rows:]
        for d in range(2):
            fsend[t, d] = f[d * block_rows : (d + 1) * block_rows]
            to = at * 2 + d

            @pl.when(to != me)
            def _():
                rdma(fsend.at[t, d], frecv.at[me], f_send.at[t, d], f_recv.at[me], {"chol": to}).start()

        return carry

    lax.fori_loop(0, n_chunks, fock, 0)

    result = fsend[n_chunks - 1, y]
    for k in range(1, n_chol):
        source = lax.rem(me + k, n_chol)
        rdma(frecv.at[source], frecv.at[source], f_send.at[0, 0], f_recv.at[source], sibling).wait_recv()
        result = result + frecv[source]
    out_ref[...] = result

    weights.wait_send()

    @pl.when(line(z - step))
    def _():
        rdma(th.at[w, me], th.at[w, me], z_send.at[n_chol], th_recv.at[w, me], peer).wait_send()

    pass_on(me, z_send, peer).wait_send()

    def drain_theta(at, carry):
        for d in range(2):
            pass_on(at * 2 + d, c_send, sibling).wait_send()
        pass_on(at * 2 + y, y_send, peer).wait_send()
        onward = jnp.where(at > z, z - 1, z + 1)

        @pl.when(jnp.logical_and(at != z, line(onward)))
        def _():
            pass_on(at * 2 + y, z_send, peer).wait_send()

        return carry

    lax.fori_loop(0, n_hi, drain_theta, 0)

    def drain(t, carry):
        at = lax.rem(z + 1 + t, n_hi)
        for q in range(n_groups):
            rdma(sbuf.at[t, q], rbuf.at[t, q], x_send.at[t, q], x_recv.at[t, q], peer).wait_send()
        for d in range(2):

            @pl.when(at * 2 + d != me)
            def _():
                rdma(fsend.at[t, d], frecv.at[me], f_send.at[t, d], f_recv.at[me], peer).wait_send()

        return carry

    lax.fori_loop(0, n_chunks, drain, 0)


def fused(n_chol, cholesky_factors, greens, walker_weights):
    vectors, occupied, orbitals = cholesky_factors.shape
    theta_rows = greens.shape[1]
    block_rows = occupied // (2 * n_chol)
    n_hi = n_chol // 2
    n_groups = n_hi // 2
    rows = vectors * 2 * block_rows
    width = 4 * theta_rows
    dma = pltpu.SemaphoreType.DMA
    return pl.pallas_call(
        functools.partial(exchange_kernel, (n_chol, vectors, occupied, block_rows)),
        out_shape=jax.ShapeDtypeStruct((block_rows, orbitals), jnp.float32),
        in_specs=[
            pl.BlockSpec(memory_space=pl.ANY),
            pl.BlockSpec(memory_space=pl.ANY),
            pl.BlockSpec(memory_space=pltpu.SMEM),
        ],
        out_specs=pl.BlockSpec(memory_space=pltpu.VMEM),
        scratch_shapes=[
            pltpu.VMEM((vectors, occupied, orbitals), jnp.bfloat16),
            pltpu.VMEM((2, n_chol, theta_rows, orbitals), jnp.bfloat16),
            pltpu.VMEM((2, 8, 128), jnp.float32),
            pltpu.VMEM((n_hi, n_groups, rows, width), jnp.float32),
            pltpu.VMEM((n_hi, n_groups, rows, width), jnp.bfloat16),
            pltpu.VMEM((n_hi, n_groups, rows, width), jnp.bfloat16),
            pltpu.VMEM((n_hi, 2, block_rows, orbitals), jnp.float32),
            pltpu.VMEM((n_chol, block_rows, orbitals), jnp.float32),
            dma((3,)),
            dma((2,)),
            dma((n_chol + 1,)),
            dma((n_chol,)),
            dma((n_chol,)),
            dma((2, n_chol)),
            dma((n_hi, n_groups)),
            dma((n_hi, n_groups)),
            dma((n_hi, 2)),
            dma((n_chol,)),
        ],
        compiler_params=pltpu.CompilerParams(collective_id=0, has_side_effects=True),
    )(cholesky_factors, greens, walker_weights)


def plain(cholesky_factors, greens, walker_weights):
    panel_sum_terms = jnp.einsum(
        "gnp,mp->gnm",
        cholesky_factors,
        lax.all_gather(greens[0], "chol", axis=0, tiled=True),
        preferred_element_type=jnp.float32,
    )
    margin = lax.psum(panel_sum_terms, "slab").astype(jnp.bfloat16)
    terms = jnp.einsum("gnm,gmp->np", margin, cholesky_factors, preferred_element_type=jnp.float32)
    weighted = walker_weights[0] * terms
    return lax.psum_scatter(weighted, ("walker", "chol"), scatter_dimension=0, tiled=True)


def solution(mesh):
    walkers, slabs, n_chol = (mesh.shape[axis] for axis in ("walker", "slab", "chol"))

    def per_device(cholesky_factors, greens, walker_weights):
        occupied = cholesky_factors.shape[1]
        pair = walkers == 2 and slabs == 2 and greens.shape[0] == 1
        fits = n_chol % 4 == 0 and occupied % (16 * n_chol) == 0 and 4 * greens.shape[1] % 128 == 0
        if pair and fits:
            return fused(n_chol, cholesky_factors, greens, walker_weights)
        return plain(cholesky_factors, greens, walker_weights)

    in_specs = (P("chol", None, "slab"), P("walker", "chol", "slab"), P("walker"))
    out_specs = P(("walker", "chol"), "slab")
    return jax.shard_map(
        per_device, mesh=mesh, in_specs=in_specs, out_specs=out_specs, check_vma=False
    )
```

```python
import functools

import jax
import jax.numpy as jnp
from jax import lax
from jax.experimental import pallas as pl
from jax.experimental.pallas import tpu as pltpu
from jax.sharding import PartitionSpec as P

MESH = pl.DeviceIdType.MESH
NT = (((1,), (1,)), ((), ()))


def exchange_kernel(
    sizes, l_hbm, theta_hbm, weight_ref, out_ref,
    lv, th, wbuf, own, sbuf, rbuf, own_small, sbuf_small, rbuf_small, fsend, frecv, yrecv,
    l_sem, w_sem, z_send, y_send, c_send, th_recv, x_send, x_recv, f_send, f_recv, fy_send, fy_recv,
):
    n_chol, vectors, occupied, block_rows = sizes
    n_hi = n_chol // 2
    half = occupied // 2
    chunk_rows = 2 * block_rows
    n_chunks = n_hi
    n_groups = n_hi // 2
    w = lax.axis_index("walker")
    s = lax.axis_index("slab")
    me = lax.axis_index("chol")
    z, y = me // 2, me % 2
    step = 1 - 2 * (z % 2)
    sibling = {"walker": 1 - w}
    peer = {"slab": 1 - s}
    y_peer = {"chol": z * 2 + 1 - y}

    def partner(t):
        k = n_hi - 1 - t
        return lax.rem(z // 2 + k // 2, n_groups) * 2 + lax.rem(z + k, 2)

    def line(at):
        return jnp.logical_and(at >= 0, at < n_hi)

    def signal(to):
        pl.semaphore_signal(barrier, inc=1, device_id=to, device_id_type=MESH)

    barrier = pltpu.get_barrier_semaphore()
    signal(sibling)
    signal(y_peer)
    signal({"chol": (z + step) * 2 + y})
    signal(peer)

    @pl.when(line(z - step))
    def _():
        signal({"chol": (z - step) * 2 + y})

    mine = pl.ds(pl.multiple_of(w * half, half), half)
    other = pl.ds(pl.multiple_of((1 - w) * half, half), half)
    keep = pltpu.make_async_copy(theta_hbm.at[0], th.at[w, me], l_sem.at[2])
    load_mine = pltpu.make_async_copy(l_hbm.at[:, mine], lv.at[:, mine], l_sem.at[0])
    load_other = pltpu.make_async_copy(l_hbm.at[:, other], lv.at[:, other], l_sem.at[1])
    keep.start()
    wbuf[w] = jnp.full(wbuf.shape[1:], weight_ref[0], jnp.float32)
    keep.wait()

    pl.semaphore_wait(barrier, 4 + line(z - step).astype(jnp.int32))

    def rdma(src, dst, send, recv, to):
        return pltpu.make_async_remote_copy(
            src_ref=src, dst_ref=dst, send_sem=send, recv_sem=recv, device_id=to, device_id_type=MESH
        )

    def pass_on(block, sem, to):
        return rdma(th.at[w, block], th.at[w, block], sem.at[block], th_recv.at[w, block], to)

    def arrived(walker, block):
        rdma(th.at[walker, block], th.at[walker, block], c_send.at[0], th_recv.at[walker, block], sibling).wait_recv()

    def relay(block, onward):
        @pl.when(line(onward))
        def _():
            pass_on(block, z_send, {"chol": onward * 2 + y}).start()

        pass_on(block, y_send, y_peer).start()
        pass_on(block, c_send, sibling).start()

    def from_line(d, way):
        at = z + way * d

        @pl.when(line(at))
        def _():
            arrived(w, at * 2 + y)
            relay(at * 2 + y, z - way)

    def from_y(at):
        @pl.when(line(at))
        def _():
            arrived(w, at * 2 + 1 - y)
            pass_on(at * 2 + 1 - y, c_send, sibling).start()

    @pl.when(line(z - step))
    def _():
        rdma(th.at[w, me], th.at[w, me], z_send.at[n_chol], th_recv.at[w, me], {"chol": (z - step) * 2 + y}).start()

    relay(me, z + step)
    weights = rdma(wbuf.at[w], wbuf.at[w], w_sem.at[0], w_sem.at[1], sibling)
    weights.start()
    load_mine.start()
    load_other.start()
    from_line(1, step)
    from_line(1, -step)
    from_y(z)
    from_y(z + step)
    from_line(2, step)
    from_line(2, -step)

    def slots(unit, q):
        if isinstance(unit, tuple):
            at, to = (unit[1], q), (n_chunks - 1 + unit[1], q)
            bufs = own_small.at[at], sbuf_small.at[at], rbuf_small.at[at]
        else:
            at = to = (unit, q)
            bufs = own.at[at], sbuf.at[at], rbuf.at[at]
        return bufs + (rdma(bufs[1], bufs[2], x_send.at[to], x_recv.at[to], peer),)

    def margins(unit, q):
        if isinstance(unit, tuple):
            count = block_rows
            start = z * chunk_rows + jnp.where(unit[1] == 0, 1 - y, y) * block_rows
        else:
            count = chunk_rows
            start = partner(unit) * chunk_rows
        rows = pl.ds(pl.multiple_of(w * half + start, count), count)
        x = lv[:, rows, :].reshape(vectors * count, -1)
        theta = th[:, pl.ds(4 * q, 4)]
        width = 4 * theta.shape[2]
        both = lax.dot_general(
            x, theta.reshape(2 * width, -1), NT, preferred_element_type=jnp.float32
        )
        a = wbuf[0][:1, :1] * both[:, :width] + wbuf[1][:1, :1] * both[:, width:]
        keep_ref, send_ref, _, copy = slots(unit, q)
        keep_ref[...] = a
        send_ref[...] = a.astype(jnp.bfloat16)
        copy.start()

    def group_arrived(q):
        for k in range(4):
            arrived(1 - w, 4 * q + k)

    def big_margins(q):
        def body(t, carry):
            margins(t, q)
            return carry

        lax.fori_loop(0, n_chunks - 1, body, 0)

    def small_margins(q):
        def body(i, carry):
            margins((None, i), q)
            return carry

        lax.fori_loop(0, 2, body, 0)

    here = z // 2
    group_arrived(here)
    rdma(wbuf.at[1 - w], wbuf.at[1 - w], w_sem.at[0], w_sem.at[1], sibling).wait_recv()
    load_mine.wait()
    big_margins(here)
    for d in range(3, n_hi):
        from_line(d, step)
        from_line(d, -step)
    from_y(z - step)
    for d in range(2, n_hi):
        from_y(z + d * step)
        from_y(z - d * step)
    for k in range(1, n_groups):
        q = lax.rem(here + k, n_groups)
        group_arrived(q)
        big_margins(q)
    for k in range(n_groups):
        small_margins(lax.rem(here + k, n_groups))
    load_other.wait()

    def fock(unit, q):
        keep_ref, _, got_ref, copy = slots(unit, q)
        copy.wait_recv()
        total = keep_ref[...] + got_ref[...].astype(jnp.float32)
        count, width = total.shape[0] // vectors, total.shape[1]
        total = jnp.concatenate(
            [total[g * count : (g + 1) * count] for g in range(vectors)], axis=1
        )
        high = total.astype(jnp.bfloat16)
        low = (total - high.astype(jnp.float32)).astype(jnp.bfloat16)
        m = pl.ds(pl.multiple_of(q * width, width), width)
        both = jnp.dot(
            jnp.concatenate([high, low], axis=0),
            lv[:, m, :].reshape(vectors * width, -1),
            preferred_element_type=jnp.float32,
        )
        return both[:count] + both[count:]

    def to_y(t, d):
        return rdma(fsend.at[t, d], yrecv.at[t], fy_send.at[t], fy_recv.at[t], y_peer)

    def along_z(t):
        to = {"chol": partner(t) * 2 + y}
        return rdma(fsend.at[t, y], frecv.at[z], f_send.at[t], f_recv.at[z], to)

    def add_and_pass(t):
        to_y(t, 1 - y).wait_recv()
        fsend[t, y] = fsend[t, y] + yrecv[t]
        along_z(t).start()

    for k in range(n_groups):
        q = lax.rem(here + k, n_groups)
        first, last = k == 0, k == n_groups - 1

        def big(t, carry):
            f = fock(t, q)
            for d in range(2):
                rows = f[d * block_rows : (d + 1) * block_rows]
                fsend[t, d] = rows if first else fsend[t, d] + rows
            if last:
                to_y(t, 1 - y).start()

                @pl.when(t > 0)
                def _():
                    add_and_pass(t - 1)

            return carry

        lax.fori_loop(0, n_chunks - 1, big, 0)

    for k in range(n_groups):
        q = lax.rem(here + k, n_groups)
        first, last = k == 0, k == n_groups - 1

        def small(i, carry):
            rows = fock((None, i), q)
            fsend[n_chunks - 1, i] = rows if first else fsend[n_chunks - 1, i] + rows
            if last:

                @pl.when(i == 0)
                def _():
                    to_y(n_chunks - 1, 0).start()
                    add_and_pass(n_chunks - 2)

            return carry

        lax.fori_loop(0, 2, small, 0)

    result = fsend[n_chunks - 1, 1]
    for k in range(1, n_hi):
        source = lax.rem(z + k, n_hi)
        rdma(frecv.at[source], frecv.at[source], f_send.at[0], f_recv.at[source], sibling).wait_recv()
        result = result + frecv[source]
    to_y(n_chunks - 1, 0).wait_recv()
    result = result + yrecv[n_chunks - 1]
    out_ref[...] = result

    weights.wait_send()

    @pl.when(line(z - step))
    def _():
        rdma(th.at[w, me], th.at[w, me], z_send.at[n_chol], th_recv.at[w, me], peer).wait_send()

    pass_on(me, z_send, peer).wait_send()

    def drain_theta(at, carry):
        for d in range(2):
            pass_on(at * 2 + d, c_send, sibling).wait_send()
        pass_on(at * 2 + y, y_send, peer).wait_send()
        onward = jnp.where(at > z, z - 1, z + 1)

        @pl.when(jnp.logical_and(at != z, line(onward)))
        def _():
            pass_on(at * 2 + y, z_send, peer).wait_send()

        return carry

    lax.fori_loop(0, n_hi, drain_theta, 0)

    def drain(t, carry):
        for q in range(n_groups):
            slots(t, q)[3].wait_send()
        to_y(t, 1 - y).wait_send()
        along_z(t).wait_send()
        return carry

    lax.fori_loop(0, n_chunks - 1, drain, 0)
    for i in range(2):
        for q in range(n_groups):
            slots((None, i), q)[3].wait_send()
    to_y(n_chunks - 1, 0).wait_send()


def fused(n_chol, cholesky_factors, greens, walker_weights):
    vectors, occupied, orbitals = cholesky_factors.shape
    theta_rows = greens.shape[1]
    block_rows = occupied // (2 * n_chol)
    n_hi = n_chol // 2
    n_groups = n_hi // 2
    rows = vectors * 2 * block_rows
    width = 4 * theta_rows
    dma = pltpu.SemaphoreType.DMA
    return pl.pallas_call(
        functools.partial(exchange_kernel, (n_chol, vectors, occupied, block_rows)),
        out_shape=jax.ShapeDtypeStruct((block_rows, orbitals), jnp.float32),
        in_specs=[
            pl.BlockSpec(memory_space=pl.ANY),
            pl.BlockSpec(memory_space=pl.ANY),
            pl.BlockSpec(memory_space=pltpu.SMEM),
        ],
        out_specs=pl.BlockSpec(memory_space=pltpu.VMEM),
        scratch_shapes=[
            pltpu.VMEM((vectors, occupied, orbitals), jnp.bfloat16),
            pltpu.VMEM((2, n_chol, theta_rows, orbitals), jnp.bfloat16),
            pltpu.VMEM((2, 8, 128), jnp.float32),
            pltpu.VMEM((n_hi - 1, n_groups, rows, width), jnp.float32),
            pltpu.VMEM((n_hi - 1, n_groups, rows, width), jnp.bfloat16),
            pltpu.VMEM((n_hi - 1, n_groups, rows, width), jnp.bfloat16),
            pltpu.VMEM((2, n_groups, rows // 2, width), jnp.float32),
            pltpu.VMEM((2, n_groups, rows // 2, width), jnp.bfloat16),
            pltpu.VMEM((2, n_groups, rows // 2, width), jnp.bfloat16),
            pltpu.VMEM((n_hi, 2, block_rows, orbitals), jnp.float32),
            pltpu.VMEM((n_hi, block_rows, orbitals), jnp.float32),
            pltpu.VMEM((n_hi, block_rows, orbitals), jnp.float32),
            dma((3,)),
            dma((2,)),
            dma((n_chol + 1,)),
            dma((n_chol,)),
            dma((n_chol,)),
            dma((2, n_chol)),
            dma((n_hi + 1, n_groups)),
            dma((n_hi + 1, n_groups)),
            dma((n_hi,)),
            dma((n_hi,)),
            dma((n_hi,)),
            dma((n_hi,)),
        ],
        compiler_params=pltpu.CompilerParams(collective_id=0, has_side_effects=True),
    )(cholesky_factors, greens, walker_weights)


def plain(cholesky_factors, greens, walker_weights):
    panel_sum_terms = jnp.einsum(
        "gnp,mp->gnm",
        cholesky_factors,
        lax.all_gather(greens[0], "chol", axis=0, tiled=True),
        preferred_element_type=jnp.float32,
    )
    margin = lax.psum(panel_sum_terms, "slab").astype(jnp.bfloat16)
    terms = jnp.einsum("gnm,gmp->np", margin, cholesky_factors, preferred_element_type=jnp.float32)
    weighted = walker_weights[0] * terms
    return lax.psum_scatter(weighted, ("walker", "chol"), scatter_dimension=0, tiled=True)


def solution(mesh):
    walkers, slabs, n_chol = (mesh.shape[axis] for axis in ("walker", "slab", "chol"))

    def per_device(cholesky_factors, greens, walker_weights):
        occupied = cholesky_factors.shape[1]
        pair = walkers == 2 and slabs == 2 and greens.shape[0] == 1
        fits = n_chol % 4 == 0 and occupied % (16 * n_chol) == 0 and 4 * greens.shape[1] % 128 == 0
        if pair and fits:
            return fused(n_chol, cholesky_factors, greens, walker_weights)
        return plain(cholesky_factors, greens, walker_weights)

    in_specs = (P("chol", None, "slab"), P("walker", "chol", "slab"), P("walker"))
    out_specs = P(("walker", "chol"), "slab")
    return jax.shard_map(
        per_device, mesh=mesh, in_specs=in_specs, out_specs=out_specs, check_vma=False
    )
```

```python
import functools

import jax
import jax.numpy as jnp
from jax import lax
from jax.experimental import pallas as pl
from jax.experimental.pallas import tpu as pltpu
from jax.sharding import PartitionSpec as P

MESH = pl.DeviceIdType.MESH
NT = (((1,), (1,)), ((), ()))


def exchange_kernel(
    sizes, l_hbm, theta_hbm, weight_ref, out_ref,
    lv, th, wbuf, own, sbuf, rbuf, own_small, sbuf_small, rbuf_small, fsend, frecv, yrecv,
    l_sem, w_sem, z_send, y_send, c_send, th_recv, x_send, x_recv, f_send, f_recv, fy_send, fy_recv,
):
    n_chol, vectors, occupied, block_rows = sizes
    n_hi = n_chol // 2
    half = occupied // 2
    chunk_rows = 2 * block_rows
    n_chunks = n_hi
    n_groups = n_hi // 2
    w = lax.axis_index("walker")
    s = lax.axis_index("slab")
    me = lax.axis_index("chol")
    z, y = me // 2, me % 2
    step = 1 - 2 * (z % 2)
    sibling = {"walker": 1 - w}
    peer = {"slab": 1 - s}
    y_peer = {"chol": z * 2 + 1 - y}

    def partner(t):
        k = n_hi - 1 - t
        return lax.rem(z // 2 + k // 2, n_groups) * 2 + lax.rem(z + k, 2)

    def line(at):
        return jnp.logical_and(at >= 0, at < n_hi)

    def signal(to):
        pl.semaphore_signal(barrier, inc=1, device_id=to, device_id_type=MESH)

    barrier = pltpu.get_barrier_semaphore()
    signal(sibling)
    signal(y_peer)
    signal({"chol": (z + step) * 2 + y})
    signal(peer)

    @pl.when(line(z - step))
    def _():
        signal({"chol": (z - step) * 2 + y})

    mine = pl.ds(pl.multiple_of(w * half, half), half)
    other = pl.ds(pl.multiple_of((1 - w) * half, half), half)
    keep = pltpu.make_async_copy(theta_hbm.at[0], th.at[w, me], l_sem.at[2])
    load_mine = pltpu.make_async_copy(l_hbm.at[:, mine], lv.at[:, mine], l_sem.at[0])
    load_other = pltpu.make_async_copy(l_hbm.at[:, other], lv.at[:, other], l_sem.at[1])
    keep.start()
    wbuf[w] = jnp.full(wbuf.shape[1:], weight_ref[0], jnp.float32)
    keep.wait()

    pl.semaphore_wait(barrier, 4 + line(z - step).astype(jnp.int32))

    def rdma(src, dst, send, recv, to):
        return pltpu.make_async_remote_copy(
            src_ref=src, dst_ref=dst, send_sem=send, recv_sem=recv, device_id=to, device_id_type=MESH
        )

    def pass_on(block, sem, to):
        return rdma(th.at[w, block], th.at[w, block], sem.at[block], th_recv.at[w, block], to)

    def arrived(walker, block):
        rdma(th.at[walker, block], th.at[walker, block], c_send.at[0], th_recv.at[walker, block], sibling).wait_recv()

    def relay(block, onward):
        @pl.when(line(onward))
        def _():
            pass_on(block, z_send, {"chol": onward * 2 + y}).start()

        pass_on(block, y_send, y_peer).start()
        pass_on(block, c_send, sibling).start()

    def from_line(d, way):
        at = z + way * d

        @pl.when(line(at))
        def _():
            arrived(w, at * 2 + y)
            relay(at * 2 + y, z - way)

    def from_y(at):
        @pl.when(line(at))
        def _():
            arrived(w, at * 2 + 1 - y)
            pass_on(at * 2 + 1 - y, c_send, sibling).start()

    @pl.when(line(z - step))
    def _():
        rdma(th.at[w, me], th.at[w, me], z_send.at[n_chol], th_recv.at[w, me], {"chol": (z - step) * 2 + y}).start()

    relay(me, z + step)
    weights = rdma(wbuf.at[w], wbuf.at[w], w_sem.at[0], w_sem.at[1], sibling)
    weights.start()
    load_mine.start()
    load_other.start()
    from_line(1, step)
    from_line(1, -step)
    from_y(z)
    from_y(z + step)
    from_line(2, step)
    from_line(2, -step)

    def slots(unit, q):
        if isinstance(unit, tuple):
            at, to = (unit[1], q), (n_chunks - 1 + unit[1], q)
            bufs = own_small.at[at], sbuf_small.at[at], rbuf_small.at[at]
        else:
            at = to = (unit, q)
            bufs = own.at[at], sbuf.at[at], rbuf.at[at]
        return bufs + (rdma(bufs[1], bufs[2], x_send.at[to], x_recv.at[to], peer),)

    def margins(unit, q):
        if isinstance(unit, tuple):
            count = block_rows
            start = z * chunk_rows + jnp.where(unit[1] == 0, 1 - y, y) * block_rows
        else:
            count = chunk_rows
            start = partner(unit) * chunk_rows
        rows = pl.ds(pl.multiple_of(w * half + start, count), count)
        x = lv[:, rows, :].reshape(vectors * count, -1)
        theta = th[:, pl.ds(4 * q, 4)]
        width = 4 * theta.shape[2]
        both = lax.dot_general(
            x, theta.reshape(2 * width, -1), NT, preferred_element_type=jnp.float32
        )
        a = wbuf[0][:1, :1] * both[:, :width] + wbuf[1][:1, :1] * both[:, width:]
        keep_ref, send_ref, _, copy = slots(unit, q)
        keep_ref[...] = a
        send_ref[...] = a.astype(jnp.bfloat16)
        copy.start()

    def group_arrived(q):
        for k in range(4):
            arrived(1 - w, 4 * q + k)

    def big_margins(q):
        def body(t, carry):
            margins(t, q)
            return carry

        lax.fori_loop(0, n_chunks - 1, body, 0)

    def small_margins(q):
        def body(i, carry):
            margins((None, i), q)
            return carry

        lax.fori_loop(0, 2, body, 0)

    here = z // 2
    group_arrived(here)
    rdma(wbuf.at[1 - w], wbuf.at[1 - w], w_sem.at[0], w_sem.at[1], sibling).wait_recv()
    load_mine.wait()
    big_margins(here)
    for d in range(3, n_hi):
        from_line(d, step)
        from_line(d, -step)
    from_y(z - step)
    for d in range(2, n_hi):
        from_y(z + d * step)
        from_y(z - d * step)
    for k in range(1, n_groups):
        q = lax.rem(here + k, n_groups)
        group_arrived(q)
        big_margins(q)
    for k in range(n_groups):
        small_margins(lax.rem(here + k, n_groups))
    load_other.wait()

    def fock(unit, q):
        keep_ref, _, got_ref, copy = slots(unit, q)
        copy.wait_recv()
        total = keep_ref[...] + got_ref[...].astype(jnp.float32)
        count, width = total.shape[0] // vectors, total.shape[1]
        total = jnp.concatenate(
            [total[g * count : (g + 1) * count] for g in range(vectors)], axis=1
        )
        high = total.astype(jnp.bfloat16)
        low = (total - high.astype(jnp.float32)).astype(jnp.bfloat16)
        m = pl.ds(pl.multiple_of(q * width, width), width)
        both = jnp.dot(
            jnp.concatenate([high, low], axis=0),
            lv[:, m, :].reshape(vectors * width, -1),
            preferred_element_type=jnp.float32,
        )
        return both[:count] + both[count:]

    def to_y(t, d):
        to = {"chol": jnp.where(t == n_chunks - 2, partner(t), z) * 2 + 1 - y}
        return rdma(fsend.at[t, d], yrecv.at[t], fy_send.at[t], fy_recv.at[t], to)

    def along_z(t):
        to = {"chol": partner(t) * 2 + y}
        return rdma(fsend.at[t, y], frecv.at[z], f_send.at[t], f_recv.at[z], to)

    def add_and_pass(t):
        to_y(t, 1 - y).wait_recv()
        fsend[t, y] = fsend[t, y] + yrecv[t]
        along_z(t).start()

    for k in range(n_groups):
        q = lax.rem(here + k, n_groups)
        first, last = k == 0, k == n_groups - 1

        def big(t, carry):
            f = fock(t, q)
            for d in range(2):
                rows = f[d * block_rows : (d + 1) * block_rows]
                fsend[t, d] = rows if first else fsend[t, d] + rows
            if last:
                to_y(t, 1 - y).start()

                @pl.when(t == n_chunks - 2)
                def _():
                    along_z(t).start()

                @pl.when(t > 0)
                def _():
                    add_and_pass(t - 1)

            return carry

        lax.fori_loop(0, n_chunks - 1, big, 0)

    for k in range(n_groups):
        q = lax.rem(here + k, n_groups)
        first, last = k == 0, k == n_groups - 1

        def small(i, carry):
            rows = fock((None, i), q)
            fsend[n_chunks - 1, i] = rows if first else fsend[n_chunks - 1, i] + rows
            if last:

                @pl.when(i == 0)
                def _():
                    to_y(n_chunks - 1, 0).start()

            return carry

        lax.fori_loop(0, 2, small, 0)

    result = fsend[n_chunks - 1, 1]
    for k in range(1, n_hi):
        source = lax.rem(z + k, n_hi)
        rdma(frecv.at[source], frecv.at[source], f_send.at[0], f_recv.at[source], sibling).wait_recv()
        result = result + frecv[source]
    for t in (n_chunks - 2, n_chunks - 1):
        to_y(t, 0).wait_recv()
        result = result + yrecv[t]
    out_ref[...] = result

    weights.wait_send()

    @pl.when(line(z - step))
    def _():
        rdma(th.at[w, me], th.at[w, me], z_send.at[n_chol], th_recv.at[w, me], peer).wait_send()

    pass_on(me, z_send, peer).wait_send()

    def drain_theta(at, carry):
        for d in range(2):
            pass_on(at * 2 + d, c_send, sibling).wait_send()
        pass_on(at * 2 + y, y_send, peer).wait_send()
        onward = jnp.where(at > z, z - 1, z + 1)

        @pl.when(jnp.logical_and(at != z, line(onward)))
        def _():
            pass_on(at * 2 + y, z_send, peer).wait_send()

        return carry

    lax.fori_loop(0, n_hi, drain_theta, 0)

    def drain(t, carry):
        for q in range(n_groups):
            slots(t, q)[3].wait_send()
        to_y(t, 1 - y).wait_send()
        along_z(t).wait_send()
        return carry

    lax.fori_loop(0, n_chunks - 1, drain, 0)
    for i in range(2):
        for q in range(n_groups):
            slots((None, i), q)[3].wait_send()
    to_y(n_chunks - 1, 0).wait_send()


def fused(n_chol, cholesky_factors, greens, walker_weights):
    vectors, occupied, orbitals = cholesky_factors.shape
    theta_rows = greens.shape[1]
    block_rows = occupied // (2 * n_chol)
    n_hi = n_chol // 2
    n_groups = n_hi // 2
    rows = vectors * 2 * block_rows
    width = 4 * theta_rows
    dma = pltpu.SemaphoreType.DMA
    return pl.pallas_call(
        functools.partial(exchange_kernel, (n_chol, vectors, occupied, block_rows)),
        out_shape=jax.ShapeDtypeStruct((block_rows, orbitals), jnp.float32),
        in_specs=[
            pl.BlockSpec(memory_space=pl.ANY),
            pl.BlockSpec(memory_space=pl.ANY),
            pl.BlockSpec(memory_space=pltpu.SMEM),
        ],
        out_specs=pl.BlockSpec(memory_space=pltpu.VMEM),
        scratch_shapes=[
            pltpu.VMEM((vectors, occupied, orbitals), jnp.bfloat16),
            pltpu.VMEM((2, n_chol, theta_rows, orbitals), jnp.bfloat16),
            pltpu.VMEM((2, 8, 128), jnp.float32),
            pltpu.VMEM((n_hi - 1, n_groups, rows, width), jnp.float32),
            pltpu.VMEM((n_hi - 1, n_groups, rows, width), jnp.bfloat16),
            pltpu.VMEM((n_hi - 1, n_groups, rows, width), jnp.bfloat16),
            pltpu.VMEM((2, n_groups, rows // 2, width), jnp.float32),
            pltpu.VMEM((2, n_groups, rows // 2, width), jnp.bfloat16),
            pltpu.VMEM((2, n_groups, rows // 2, width), jnp.bfloat16),
            pltpu.VMEM((n_hi, 2, block_rows, orbitals), jnp.float32),
            pltpu.VMEM((n_hi, block_rows, orbitals), jnp.float32),
            pltpu.VMEM((n_hi, block_rows, orbitals), jnp.float32),
            dma((3,)),
            dma((2,)),
            dma((n_chol + 1,)),
            dma((n_chol,)),
            dma((n_chol,)),
            dma((2, n_chol)),
            dma((n_hi + 1, n_groups)),
            dma((n_hi + 1, n_groups)),
            dma((n_hi,)),
            dma((n_hi,)),
            dma((n_hi,)),
            dma((n_hi,)),
        ],
        compiler_params=pltpu.CompilerParams(collective_id=0, has_side_effects=True),
    )(cholesky_factors, greens, walker_weights)


def plain(cholesky_factors, greens, walker_weights):
    panel_sum_terms = jnp.einsum(
        "gnp,mp->gnm",
        cholesky_factors,
        lax.all_gather(greens[0], "chol", axis=0, tiled=True),
        preferred_element_type=jnp.float32,
    )
    margin = lax.psum(panel_sum_terms, "slab").astype(jnp.bfloat16)
    terms = jnp.einsum("gnm,gmp->np", margin, cholesky_factors, preferred_element_type=jnp.float32)
    weighted = walker_weights[0] * terms
    return lax.psum_scatter(weighted, ("walker", "chol"), scatter_dimension=0, tiled=True)


def solution(mesh):
    walkers, slabs, n_chol = (mesh.shape[axis] for axis in ("walker", "slab", "chol"))

    def per_device(cholesky_factors, greens, walker_weights):
        occupied = cholesky_factors.shape[1]
        pair = walkers == 2 and slabs == 2 and greens.shape[0] == 1
        fits = n_chol % 4 == 0 and occupied % (16 * n_chol) == 0 and 4 * greens.shape[1] % 128 == 0
        if pair and fits:
            return fused(n_chol, cholesky_factors, greens, walker_weights)
        return plain(cholesky_factors, greens, walker_weights)

    in_specs = (P("chol", None, "slab"), P("walker", "chol", "slab"), P("walker"))
    out_specs = P(("walker", "chol"), "slab")
    return jax.shard_map(
        per_device, mesh=mesh, in_specs=in_specs, out_specs=out_specs, check_vma=False
    )
```
